768 devices in a mesh: space: 12 (over z_lo, core), frame: 64 (over z_hi, y, x).
Axes of the slice: x: 4, y: 8, z: 12 (z_hi: 2, z_lo: 6; z = z_hi * 6 + z_lo), core: 2. Of those that a mesh axis runs over, the one named last changes fastest.
Arguments:
- latent: bfloat16 [64, 6144, 1024], P('frame', 'space'), may hold values from -6 to 6
- cond: float32 [3, 1024], replicated, may hold values from -3 to 3
- w_qkv: bfloat16 [1024, 3072], replicated
- w_out: bfloat16 [1024, 1024], replicated, may hold values from -0.1875 to 0.1875
- slot: int32 [6144], P('space'), may hold values from 0 to 511, as said below
- neighbours: int32 [48, 4], P('space'), may hold values from 0 to 47, as said below
- counts: int32 [48], P('space'), may hold values from 1 to 4
Outputs:
- updated: bfloat16 [64, 6144, 1024], P('frame', 'space')
The draws below stay inside these ranges and needn't reach their ends.
Inputs may be any that keep to these rules, and one draw needn't show every extreme that they name: `slot`: each aligned group of 512 entries is a permutation of its range. `neighbours`: row b lists distinct blocks (b + o) mod 48 with -4 <= o <= 4, the first being b itself.
All inputs are finite; a program needn't handle non-finite values.
Results may differ from the reference program's by a relative error of at most 0.0052.
Values may be sent and summed in bfloat16 or wider, within the bound.
No kernel may reach another device: no remote copies, remote signals or barrier semaphores. Data moves between devices by JAX's collectives and lax.ppermute only.
A program may use at most 64 MiB of HBM per device.

```python
import jax
import jax.numpy as jnp
from jax import lax

D = 1024
HEADS = 8
BLOCK = 128
MAXNB = 4
BLK_DEV = 4
TOK_DEV = 512
NBLK = 48
NTOK = 6144
FRAMES = 64
CLIP = 8


def draw_w_qkv(key, part):
    first = jax.random.fold_in(key, 0)
    base = jax.random.normal(first, (D, 3 * D), jnp.float32) / jnp.sqrt(jnp.float32(D))
    return base.astype(jnp.bfloat16)


def draw_slot(key, part):
    groups = jax.random.split(key, NTOK // TOK_DEV)
    perms = jax.vmap(lambda k: jax.random.permutation(k, TOK_DEV))(groups)
    return perms.reshape(-1).astype(jnp.int32)


def draw_neighbours(key, part):
    rows = jax.random.split(jax.random.fold_in(key, 11), NBLK)
    picks = jax.vmap(lambda k: jax.random.permutation(k, 2 * BLK_DEV)[:MAXNB - 1])(rows)
    offsets = jnp.concatenate([jnp.arange(-BLK_DEV, 0, dtype=jnp.int32), jnp.arange(1, BLK_DEV + 1, dtype=jnp.int32)])
    chosen = jnp.concatenate([jnp.zeros((NBLK, 1), jnp.int32), offsets[picks]], axis=1)
    return jnp.mod(jnp.arange(NBLK, dtype=jnp.int32)[:, None] + chosen, NBLK).astype(jnp.int32)


def draw_counts(key, part):
    first, second = jax.random.split(jax.random.fold_in(key, 23))
    device_top = jax.random.randint(first, (NBLK // BLK_DEV,), 1, MAXNB + 1)
    tops = jnp.repeat(device_top, BLK_DEV)
    drawn = jax.random.randint(second, (NBLK,), 1, tops + 1)
    return drawn.at[0].set(MAXNB).astype(jnp.int32)


def levels(own_key, dims, pieces, smallest, largest):
    def one(axis_at, shards_of):
        steps = jax.random.uniform(jax.random.fold_in(jax.random.fold_in(own_key, 6), axis_at), (shards_of,), jnp.float32, smallest / len(pieces), largest / len(pieces))
        return jnp.repeat(jnp.exp(steps), dims[axis_at] // shards_of).reshape((-1,) + (1,) * (len(dims) - axis_at - 1))

    level = one(*pieces[0])
    for cut in pieces[1:]:
        level = level * one(*cut)
    return level


def normal_values(key, extent, width, most, shards=(), kind=jnp.bfloat16):
    array = jax.random.normal(key, extent, jnp.float32) * width
    if len(shards) > 0:
        array = levels(key, extent, shards, -0.22, 0.18) * array
    return jnp.clip(array, min=-most, max=most).astype(kind)


def setup_inputs(seed: int = 0) -> dict:
    key_list = jax.random.split(jax.random.key(seed), 8)
    latent = normal_values(key_list[0], (FRAMES, NTOK, D), 1.0, 6.0, ((0, 64), (1, 12)))
    cond = normal_values(key_list[1], (3, D), 0.7, 3.0, (), jnp.float32)
    w_qkv = draw_w_qkv(jax.random.fold_in(key_list[7], 71), 0)
    w_out = normal_values(key_list[3], (D, D), D ** -0.5, 0.1875)
    slot = draw_slot(jax.random.fold_in(key_list[7], 71), 0)
    neighbours = draw_neighbours(jax.random.fold_in(key_list[7], 71), 0)
    counts = draw_counts(jax.random.fold_in(key_list[7], 71), 0)
    return dict(latent=latent, cond=cond, w_qkv=w_qkv, w_out=w_out, slot=slot, neighbours=neighbours, counts=counts)


def softmax_last(scores):
    top = lax.optimization_barrier(jnp.max(scores, axis=-1, keepdims=True))
    expo = jnp.exp(scores - top)
    return expo / lax.optimization_barrier(jnp.sum(expo, axis=-1, keepdims=True))

def reference(latent, cond, w_qkv, w_out, slot, neighbours, counts):
    head_dim = D // HEADS
    sheads = HEADS // 2
    half = D // 2
    scale = 1.0 / jnp.sqrt(jnp.float32(head_dim))
    x_full = latent.astype(jnp.float32)

    def project(frame_rows):
        centred = frame_rows - lax.optimization_barrier(jnp.mean(frame_rows, axis=-1, keepdims=True))
        normed = centred * lax.rsqrt(lax.optimization_barrier(jnp.mean(centred * centred, axis=-1, keepdims=True)) + 1e-06)
        modulated = (normed * (1.0 + cond[1]) + cond[0]).astype(jnp.bfloat16)
        return jnp.dot(modulated, w_qkv, preferred_element_type=jnp.float32).astype(jnp.bfloat16)
    projected = lax.map(project, x_full)
    order = jnp.arange(NTOK, dtype=jnp.int32) // TOK_DEV * TOK_DEV + slot.astype(jnp.int32)
    valid = jnp.arange(MAXNB, dtype=jnp.int32)[None, :] < counts[:, None]

    def spatial_frame(proj):
        ranked = proj[order]
        q_blocks = ranked[:, :half].reshape(NBLK, BLOCK, sheads, head_dim)
        k_blocks = ranked[:, D:D + half].reshape(NBLK, BLOCK, sheads, head_dim)
        v_blocks = ranked[:, 2 * D:2 * D + half].reshape(NBLK, BLOCK, sheads, head_dim)

        def one_block(items):
            query, ids, usable = items
            keys = k_blocks[ids].reshape(MAXNB * BLOCK, sheads, head_dim).astype(jnp.float32)
            vals = v_blocks[ids].reshape(MAXNB * BLOCK, sheads, head_dim).astype(jnp.float32)
            scores = jnp.einsum('qhd,khd->hqk', query.astype(jnp.float32), keys, precision=lax.Precision.HIGHEST) * scale
            keep = jnp.repeat(usable, BLOCK)[None, None, :]
            scores = jnp.where(keep, scores, -jnp.inf)
            weights = softmax_last(scores).astype(jnp.bfloat16).astype(jnp.float32)
            result = jnp.einsum('hqk,khd->qhd', weights, vals, precision=lax.Precision.HIGHEST)
            return result.astype(jnp.bfloat16).reshape(BLOCK, half)
        block_out = lax.map(one_block, (q_blocks, neighbours, valid)).reshape(NTOK, half)
        return jnp.zeros((NTOK, half), jnp.bfloat16).at[order].set(block_out)
    spatial = lax.map(spatial_frame, projected)
    clip_of = jnp.arange(FRAMES, dtype=jnp.int32) // CLIP
    same_clip = clip_of[:, None] == clip_of[None, :]

    def temporal_head(head):
        lo = half + head * head_dim
        t_query = lax.dynamic_slice_in_dim(projected, lo, head_dim, 2).astype(jnp.float32)
        t_key = lax.dynamic_slice_in_dim(projected, D + lo, head_dim, 2).astype(jnp.float32)
        t_val = lax.dynamic_slice_in_dim(projected, 2 * D + lo, head_dim, 2).astype(jnp.float32)
        t_scores = jnp.einsum('ftd,gtd->tfg', t_query, t_key, precision=lax.Precision.HIGHEST) * scale
        t_scores = jnp.where(same_clip[None], t_scores, -jnp.inf)
        t_weights = softmax_last(t_scores)
        result = jnp.einsum('tfg,gtd->ftd', t_weights, t_val, precision=lax.Precision.HIGHEST)
        return result.astype(jnp.bfloat16)
    per_head = lax.map(temporal_head, jnp.arange(sheads, dtype=jnp.int32))
    temporal = jnp.transpose(per_head, (1, 2, 0, 3)).reshape(FRAMES, NTOK, half)
    joined = jnp.concatenate([spatial, temporal], axis=-1)

    def finish(items):
        heads_out, rows = items
        mixed = jnp.dot(heads_out, w_out, preferred_element_type=jnp.float32)
        return (rows + cond[2] * mixed).astype(jnp.bfloat16)
    return lax.map(finish, (joined, x_full))
```

```python
import jax
import jax.numpy as jnp
from jax import lax
from jax.experimental import pallas as pl
from jax.experimental.pallas import tpu as pltpu
from jax.sharding import Mesh, PartitionSpec as P

HEADS = 8
SHEADS = 4
HD = 128
MAXNB = 4
BLK = 128
NB = 4
CLIP = 8
EPS = 1e-06
NEG = -1e30
F32 = jnp.float32
BF16 = jnp.bfloat16


def dot(a, b):
    return jnp.dot(a, b, preferred_element_type=F32)


def dot_t(a, b):
    return lax.dot_general(a, b, (((1,), (1,)), ((), ())), preferred_element_type=F32)


def modulate(rows, shift, gain):
    mean = jnp.mean(rows, axis=-1, keepdims=True)
    centred = rows - mean
    var = jnp.mean(centred * centred, axis=-1, keepdims=True)
    return (centred * lax.rsqrt(var + EPS) * gain + shift).astype(BF16)


def one_hot_rows(slot_row):
    tokens = slot_row.shape[1]
    cols = jnp.broadcast_to(slot_row, (128, tokens)).T
    lane = lax.broadcasted_iota(jnp.int32, (tokens, 128), 1)
    parts = [
        (cols == lane + 128 * c).astype(F32).astype(BF16) for c in range(tokens // 128)
    ]
    return jnp.concatenate(parts, axis=1)


def spatial_project(x_hbm, cond_ref, slot_ref, w_hbm, kv_hbm, q_hbm, x_s, w_s, mod_s, kv_s, q_s, sem):
    tokens, width = x_s.shape
    half = width // 2
    x_in = pltpu.make_async_copy(x_hbm.at[0], x_s, sem.at[0])
    x_in.start()
    w_in = []
    for i, c in enumerate((width, 2 * width, 0)):
        copy = pltpu.make_async_copy(
            w_hbm.at[:, pl.ds(c, half)], w_s.at[:, pl.ds(i * half, half)], sem.at[1 + i]
        )
        copy.start()
        w_in.append(copy)
    perm = one_hot_rows(slot_ref[...])
    shift = cond_ref[0:1, :]
    gain = 1.0 + cond_ref[1:2, :]
    x_in.wait()
    for j in range(NB):
        sl = slice(j * BLK, (j + 1) * BLK)
        mod_s[sl, :] = modulate(dot(perm[sl, :], x_s[...]), shift, gain)
    outs = []
    for i in range(2):
        w_in[i].wait()
        cs = slice(i * half, (i + 1) * half)
        kv_s[:, cs] = dot(mod_s[...], w_s[:, cs]).astype(BF16)
        out = pltpu.make_async_copy(kv_s.at[:, pl.ds(i * half, half)], kv_hbm.at[:, pl.ds(i * half, half)], sem.at[4 + i])
        out.start()
        outs.append(out)
    w_in[2].wait()
    q_s[...] = dot(mod_s[...], w_s[:, 2 * half :]).astype(BF16)
    out = pltpu.make_async_copy(q_s, q_hbm, sem.at[6])
    out.start()
    outs.append(out)
    for out in outs:
        out.wait()


def temporal(x_hbm, cond_ref, w_hbm, o_ref, x_s, w_s, mod_s, p_s, sem):
    frames, count, width = x_s.shape
    half = width // 2
    rows = frames * count
    x_in = pltpu.make_async_copy(x_hbm, x_s, sem.at[0])
    x_in.start()
    w_in = []
    for i in range(3):
        copy = pltpu.make_async_copy(
            w_hbm.at[:, pl.ds(i * width + half, half)], w_s.at[:, pl.ds(i * half, half)], sem.at[1 + i]
        )
        copy.start()
        w_in.append(copy)
    shift = cond_ref[0:1, :]
    gain = 1.0 + cond_ref[1:2, :]
    x_in.wait()
    for f in range(0, frames, 2):
        piece = x_s[f : f + 2].reshape(2 * count, width).astype(F32)
        mod_s[f * count : (f + 2) * count, :] = modulate(piece, shift, gain)
    for i in range(3):
        w_in[i].wait()
        cs = slice(i * half, (i + 1) * half)
        p_s[:, :, cs] = dot(mod_s[...], w_s[:, cs]).astype(BF16).reshape(frames, count, half)
    group = 128 // frames
    scale = 1.0 / jnp.sqrt(F32(HD))
    ri = lax.broadcasted_iota(jnp.int32, (128, 128), 0) % group
    ci = lax.broadcasted_iota(jnp.int32, (128, 128), 1) % group
    same = ri == ci
    for t in range(count // group):
        ts = slice(t * group, (t + 1) * group)
        for h in range(SHEADS):
            def part(i):
                lo = i * half + h * HD
                return p_s[:, ts, lo : lo + HD].reshape(128, HD)

            s = jnp.where(same, dot_t(part(0), part(1)) * scale, NEG)
            e = jnp.exp(s - jnp.max(s, axis=-1, keepdims=True))
            w = e / jnp.sum(e, axis=-1, keepdims=True)
            hi = w.astype(BF16)
            lo = (w - hi.astype(F32)).astype(BF16)
            v = part(2)
            o = dot(hi, v) + dot(lo, v)
            o_ref[:, ts, h * HD : (h + 1) * HD] = o.astype(BF16).reshape(frames, group, HD)


def finish(nb_ref, cnt_ref, x_hbm, cond_ref, slot_ref, q_hbm, kv_hbm, left_hbm, right_hbm, t_hbm, w_hbm, o_ref,
           x_s, q_s, win, t_s, w_s, blk_s, acc_s, sem):
    tokens, width = x_s.shape
    half = width // 2
    copies = [
        (left_hbm, win.at[pl.ds(0, tokens)]),
        (kv_hbm, win.at[pl.ds(tokens, tokens)]),
        (right_hbm, win.at[pl.ds(2 * tokens, tokens)]),
        (q_hbm, q_s),
        (t_hbm, t_s),
        (w_hbm, w_s),
        (x_hbm.at[0], x_s),
    ]
    copies = [pltpu.make_async_copy(a, b, sem.at[i]) for i, (a, b) in enumerate(copies)]
    for c in copies:
        c.start()
    tok = lax.broadcasted_iota(jnp.int32, (tokens, tokens), 0)
    unperm = (tok == slot_ref[...]).astype(F32).astype(BF16)
    copies[4].wait()
    copies[5].wait()
    acc_s[...] = dot(t_s[...], w_s[half:, :])
    for i in range(4):
        copies[i].wait()
    scale = 1.0 / jnp.sqrt(F32(HD))
    first = nb_ref[0, 0]
    total = 12 * NB
    for j in range(NB):
        rows = slice(j * BLK, (j + 1) * BLK)
        starts = []
        ok = []
        for n in range(MAXNB):
            at = lax.rem(nb_ref[j, n] - first + NB + total, total)
            at = jnp.minimum(at, 3 * NB - 1)
            starts.append(pl.multiple_of(at * BLK, BLK))
            ok.append(n < cnt_ref[j])
        for h in range(SHEADS):
            q = q_s[rows, h * HD : (h + 1) * HD]
            ss = []
            for n in range(MAXNB):
                k = win[pl.ds(starts[n], BLK), h * HD : (h + 1) * HD]
                s = dot_t(q, k) * scale
                if n > 0:
                    s = jnp.where(ok[n], s, NEG)
                ss.append(s)
            top = ss[0]
            for s in ss[1:]:
                top = jnp.maximum(top, s)
            top = jnp.max(top, axis=-1, keepdims=True)
            es = [jnp.exp(s - top) for s in ss]
            tot = jnp.sum(es[0] + es[1] + es[2] + es[3], axis=-1, keepdims=True)
            inv = 1.0 / tot
            o = None
            for n in range(MAXNB):
                v = win[pl.ds(starts[n], BLK), half + h * HD : half + (h + 1) * HD]
                p = dot((es[n] * inv).astype(BF16), v)
                o = p if o is None else o + p
            blk_s[rows, h * HD : (h + 1) * HD] = o.astype(BF16)
    copies[6].wait()
    gate = cond_ref[2:3, :]
    for j in range(NB):
        rows = slice(j * BLK, (j + 1) * BLK)
        sp = dot(unperm[rows, :], blk_s[...]).astype(BF16)
        mixed = dot(sp, w_s[:half, :]) + acc_s[rows, :]
        o_ref[0, rows, :] = (x_s[rows, :].astype(F32) + gate * mixed).astype(BF16)


ANY = pl.BlockSpec(memory_space=pl.ANY)
VM = pl.BlockSpec(memory_space=pltpu.VMEM)
SM = pl.BlockSpec(memory_space=pltpu.SMEM)


def body(latent, cond, w_qkv, w_out, slot, neighbours, counts):
    tokens, width = latent.shape[1], latent.shape[2]
    half = width // 2
    per = tokens // CLIP
    slot_row = slot.reshape(1, tokens)
    seen = lax.all_to_all(latent.reshape(CLIP, per, width), "member", 0, 0, tiled=True)
    kv, q = pl.pallas_call(
        spatial_project,
        out_shape=(
            jax.ShapeDtypeStruct((tokens, width), BF16),
            jax.ShapeDtypeStruct((tokens, half), BF16),
        ),
        in_specs=[ANY, VM, VM, ANY],
        out_specs=(ANY, ANY),
        scratch_shapes=[
            pltpu.VMEM((tokens, width), BF16),
            pltpu.VMEM((width, 3 * half), BF16),
            pltpu.VMEM((tokens, width), BF16),
            pltpu.VMEM((tokens, width), BF16),
            pltpu.VMEM((tokens, half), BF16),
            pltpu.SemaphoreType.DMA((7,)),
        ],
        name="spatial_project",
    )(latent, cond, slot_row, w_qkv)
    count = lax.axis_size("space")
    left = lax.ppermute(kv, "space", [(i, (i + 1) % count) for i in range(count)])
    right = lax.ppermute(kv, "space", [((i + 1) % count, i) for i in range(count)])
    t_out = pl.pallas_call(
        temporal,
        out_shape=jax.ShapeDtypeStruct((CLIP, per, half), BF16),
        in_specs=[ANY, VM, ANY],
        out_specs=VM,
        scratch_shapes=[
            pltpu.VMEM((CLIP, per, width), BF16),
            pltpu.VMEM((width, 3 * half), BF16),
            pltpu.VMEM((tokens, width), BF16),
            pltpu.VMEM((CLIP, per, 3 * half), BF16),
            pltpu.SemaphoreType.DMA((4,)),
        ],
        name="temporal",
    )(seen, cond, w_qkv)
    back = lax.all_to_all(t_out, "member", 0, 0, tiled=True).reshape(tokens, half)
    return pl.pallas_call(
        finish,
        out_shape=jax.ShapeDtypeStruct((1, tokens, width), BF16),
        in_specs=[SM, SM, ANY, VM, VM, ANY, ANY, ANY, ANY, ANY, ANY],
        out_specs=VM,
        scratch_shapes=[
            pltpu.VMEM((tokens, width), BF16),
            pltpu.VMEM((tokens, half), BF16),
            pltpu.VMEM((3 * tokens, width), BF16),
            pltpu.VMEM((tokens, half), BF16),
            pltpu.VMEM((width, width), BF16),
            pltpu.VMEM((tokens, half), BF16),
            pltpu.VMEM((tokens, width), F32),
            pltpu.SemaphoreType.DMA((7,)),
        ],
        name="finish",
    )(neighbours, counts, latent, cond, slot_row, q, kv, left, right, back, w_out)


def solution(mesh):
    devices = mesh.devices
    spaces, frames = devices.shape
    fine = Mesh(devices.reshape(spaces, frames // CLIP, CLIP), ("space", "clip", "member"))
    whole = ("clip", "member")
    in_specs = (P(whole, "space", None), P(), P(), P(), P("space"), P("space", None), P("space"))
    out_specs = P(whole, "space", None)
    return jax.shard_map(body, mesh=fine, in_specs=in_specs, out_specs=out_specs, check_vma=False)
```

```python
import jax
import jax.numpy as jnp
from jax import lax
from jax.experimental import pallas as pl
from jax.experimental.pallas import tpu as pltpu
from jax.sharding import Mesh, PartitionSpec as P

HEADS = 8
SHEADS = 4
HD = 128
MAXNB = 4
BLK = 128
NB = 4
CLIP = 8
EPS = 1e-06
NEG = -1e30
F32 = jnp.float32
BF16 = jnp.bfloat16


def dot(a, b):
    return jnp.dot(a, b, preferred_element_type=F32)


def dot_t(a, b):
    return lax.dot_general(a, b, (((1,), (1,)), ((), ())), preferred_element_type=F32)


def modulate(rows, shift, gain):
    mean = jnp.mean(rows, axis=-1, keepdims=True)
    centred = rows - mean
    var = jnp.mean(centred * centred, axis=-1, keepdims=True)
    return (centred * lax.rsqrt(var + EPS) * gain + shift).astype(BF16)


def one_hot_rows(slot_row):
    tokens = slot_row.shape[1]
    cols = jnp.broadcast_to(slot_row, (128, tokens)).T
    lane = lax.broadcasted_iota(jnp.int32, (tokens, 128), 1)
    parts = [
        (cols == lane + 128 * c).astype(F32).astype(BF16) for c in range(tokens // 128)
    ]
    return jnp.concatenate(parts, axis=1)


def spatial_keyval(x_hbm, cond_ref, slot_ref, w_hbm, kv_hbm, mod_hbm, x_s, w_s, mod_s, kv_s, sem):
    tokens, width = x_s.shape
    half = width // 2
    x_in = pltpu.make_async_copy(x_hbm.at[0], x_s, sem.at[5])
    x_in.start()
    halves = [slice(i * half, (i + 1) * half) for i in range(2)]
    w_in = []
    for i, cs in enumerate(halves):
        copy = pltpu.make_async_copy(w_hbm.at[:, pl.ds((i + 1) * width, half)], w_s.at[:, cs], sem.at[i])
        copy.start()
        w_in.append(copy)
    perm = one_hot_rows(slot_ref[...])
    shift = cond_ref[0:1, :]
    gain = 1.0 + cond_ref[1:2, :]
    x_in.wait()
    for j in range(NB):
        sl = slice(j * BLK, (j + 1) * BLK)
        mod_s[sl, :] = modulate(dot(perm[sl, :], x_s[...]), shift, gain)
    outs = [pltpu.make_async_copy(mod_s, mod_hbm, sem.at[2])]
    outs[0].start()
    for i, cs in enumerate(halves):
        w_in[i].wait()
        kv_s[:, cs] = dot(mod_s[...], w_s[:, cs]).astype(BF16)
        out = pltpu.make_async_copy(kv_s.at[:, cs], kv_hbm.at[:, cs], sem.at[3 + i])
        out.start()
        outs.append(out)
    for out in outs:
        out.wait()


def spatial_query(mod_hbm, w_hbm, q_ref, mod_s, w_s, sem):
    half = q_ref.shape[1]
    w_in = pltpu.make_async_copy(w_hbm.at[:, pl.ds(0, half)], w_s, sem.at[0])
    m_in = pltpu.make_async_copy(mod_hbm, mod_s, sem.at[1])
    w_in.start()
    m_in.start()
    w_in.wait()
    m_in.wait()
    q_ref[...] = dot(mod_s[...], w_s[...]).astype(BF16)


def temporal(x_ref, cond_ref, w_hbm, o_hbm, w_s, mod_s, p_s, o_s, sem):
    frames, count, width = x_ref.shape
    half = width // 2
    w_in = []
    for i in range(3):
        copy = pltpu.make_async_copy(
            w_hbm.at[:, pl.ds(i * width + half, half)], w_s.at[:, pl.ds(i * half, half)], sem.at[i]
        )
        copy.start()
        w_in.append(copy)
    shift = cond_ref[0:1, :]
    gain = 1.0 + cond_ref[1:2, :]
    for f in range(0, frames, 2):
        piece = x_ref[f : f + 2].reshape(2 * count, width).astype(F32)
        mod_s[f * count : (f + 2) * count, :] = modulate(piece, shift, gain)
    for i in range(3):
        w_in[i].wait()
        cs = slice(i * half, (i + 1) * half)
        p_s[:, :, cs] = dot(mod_s[...], w_s[:, cs]).astype(BF16).reshape(frames, count, half)
    group = 128 // frames
    scale = 1.0 / jnp.sqrt(F32(HD))
    ri = lax.broadcasted_iota(jnp.int32, (128, 128), 0) % group
    ci = lax.broadcasted_iota(jnp.int32, (128, 128), 1) % group
    same = ri == ci
    outs = []
    for t in range(count // group):
        ts = slice(t * group, (t + 1) * group)

        def part(i, h):
            lo = i * half + h * HD
            return p_s[:, ts, lo : lo + HD].reshape(128, HD)

        heads = range(SHEADS)
        ss = [jnp.where(same, dot_t(part(0, h), part(1, h)) * scale, NEG) for h in heads]
        es = [jnp.exp(s - jnp.max(s, axis=-1, keepdims=True)) for s in ss]
        ws = [e * (1.0 / jnp.sum(e, axis=-1, keepdims=True)) for e in es]
        his = [w.astype(BF16) for w in ws]
        los = [(w - hi.astype(F32)).astype(BF16) for w, hi in zip(ws, his)]
        for h in heads:
            o = dot(his[h], part(2, h)) + dot(los[h], part(2, h))
            o_s[:, ts, h * HD : (h + 1) * HD] = o.astype(BF16).reshape(frames, group, HD)
        out = pltpu.make_async_copy(o_s.at[:, ts], o_hbm.at[:, ts], sem.at[3 + t])
        out.start()
        outs.append(out)
    for out in outs:
        out.wait()


def finish(nb_ref, cnt_ref, x_hbm, cond_ref, slot_ref, q_hbm, kv_hbm, left_hbm, right_hbm, t_ref, w_ref, o_hbm,
           x_s, q_ref, win, blk_s, acc_s, o_s, sem):
    tokens, width = x_s.shape
    half = width // 2
    copies = [
        (left_hbm, win.at[pl.ds(0, tokens)]),
        (right_hbm, win.at[pl.ds(2 * tokens, tokens)]),
        (kv_hbm, win.at[pl.ds(tokens, tokens)]),
        (q_hbm, q_ref),
        (x_hbm.at[0], x_s),
    ]
    copies = [pltpu.make_async_copy(a, b, sem.at[i]) for i, (a, b) in enumerate(copies)]
    for c in copies:
        c.start()
    tok = lax.broadcasted_iota(jnp.int32, (tokens, tokens), 0)
    unperm = (tok == slot_ref[...]).astype(F32).astype(BF16)
    acc_s[...] = dot(t_ref[...], w_ref[half:, :])
    scale = 1.0 / jnp.sqrt(F32(HD))
    first = nb_ref[0, 0]
    total = 12 * NB
    for c in copies[:4]:
        c.wait()
    for j in range(NB):
        rows = slice(j * BLK, (j + 1) * BLK)
        starts = []
        lane = lax.broadcasted_iota(jnp.int32, (BLK, MAXNB * BLK), 1)
        keep = lane < cnt_ref[j] * BLK
        for n in range(MAXNB):
            at = lax.rem(nb_ref[j, n] - first + NB + total, total)
            at = jnp.minimum(at, 3 * NB - 1)
            starts.append(pl.multiple_of(at * BLK, BLK))

        def listed(lo):
            return jnp.concatenate([win[pl.ds(at, BLK), lo : lo + HD] for at in starts], axis=0)

        heads = range(SHEADS)
        cols = [slice(h * HD, (h + 1) * HD) for h in heads]
        ss = [jnp.where(keep, dot_t(q_ref[rows, cols[h]], listed(h * HD)) * scale, NEG) for h in heads]
        tops = [jnp.max(s, axis=-1, keepdims=True) for s in ss]
        es = [jnp.exp(s - top) for s, top in zip(ss, tops)]
        invs = [1.0 / jnp.sum(e, axis=-1, keepdims=True) for e in es]
        ps = [(e * inv).astype(BF16) for e, inv in zip(es, invs)]
        for h in heads:
            blk_s[rows, cols[h]] = dot(ps[h], listed(half + h * HD)).astype(BF16)
    copies[4].wait()
    gate = cond_ref[2:3, :]
    outs = []
    for j in range(NB):
        rows = slice(j * BLK, (j + 1) * BLK)
        sp = dot(unperm[rows, :], blk_s[...]).astype(BF16)
        mixed = dot(sp, w_ref[:half, :]) + acc_s[rows, :]
        o_s[rows, :] = (x_s[rows, :].astype(F32) + gate * mixed).astype(BF16)
        out = pltpu.make_async_copy(o_s.at[rows], o_hbm.at[0, rows], sem.at[5 + j])
        out.start()
        outs.append(out)
    for out in outs:
        out.wait()


HB = pl.BlockSpec(memory_space=pltpu.HBM)
VM = pl.BlockSpec(memory_space=pltpu.VMEM)
SM = pl.BlockSpec(memory_space=pltpu.SMEM)
DMA = pltpu.SemaphoreType.DMA


def near(x):
    return pltpu.with_memory_space_constraint(x, pltpu.VMEM)


def call(kernel, ins, outs, shapes, scratch):
    return pl.pallas_call(
        kernel,
        out_shape=shapes,
        in_specs=ins,
        out_specs=outs,
        scratch_shapes=scratch,
        name=kernel.__name__,
    )


def body(latent, cond, w_qkv, w_out, slot, neighbours, counts):
    tokens, width = latent.shape[1], latent.shape[2]
    half = width // 2
    per = tokens // CLIP
    slot_row = slot.reshape(1, tokens)
    arr = jax.ShapeDtypeStruct
    room = lambda *shape: pltpu.VMEM(shape, BF16)
    seen = lax.all_to_all(latent.reshape(CLIP, per, width), "member", 0, 0, tiled=True)
    kv, mod = call(
        spatial_keyval,
        [HB, VM, VM, HB],
        (HB, HB),
        (arr((tokens, width), BF16), arr((tokens, width), BF16)),
        [room(tokens, width), room(width, width), room(tokens, width), room(tokens, width), DMA((6,))],
    )(latent, cond, slot_row, w_qkv)
    count = lax.axis_size("space")
    left = lax.ppermute(kv, "space", [(i, (i + 1) % count) for i in range(count)])
    right = lax.ppermute(kv, "space", [((i + 1) % count, i) for i in range(count)])
    q = call(
        spatial_query,
        [HB, HB],
        VM,
        arr((tokens, half), BF16),
        [room(tokens, width), room(width, half), DMA((2,))],
    )(mod, w_qkv)
    t_out = call(
        temporal,
        [VM, VM, HB],
        HB,
        arr((CLIP, per, half), BF16),
        [
            room(width, 3 * half),
            room(tokens, width),
            room(CLIP, per, 3 * half),
            room(CLIP, per, half),
            DMA((3 + per // (128 // CLIP),)),
        ],
    )(near(seen), cond, w_qkv)
    back = lax.all_to_all(t_out, "member", 0, 0, tiled=True).reshape(tokens, half)
    return call(
        finish,
        [SM, SM, HB, VM, VM, HB, HB, HB, HB, VM, VM],
        HB,
        arr((1, tokens, width), BF16),
        [
            room(tokens, width),
            room(tokens, half),
            room(3 * tokens, width),
            room(tokens, half),
            pltpu.VMEM((tokens, width), F32),
            room(tokens, width),
            DMA((9,)),
        ],
    )(neighbours, counts, latent, cond, slot_row, q, kv, left, right, near(back), near(w_out))


def solution(mesh):
    devices = mesh.devices
    spaces, frames = devices.shape
    fine = Mesh(devices.reshape(spaces, frames // CLIP, CLIP), ("space", "clip", "member"))
    whole = ("clip", "member")
    in_specs = (P(whole, "space", None), P(), P(), P(), P("space"), P("space", None), P("space"))
    out_specs = P(whole, "space", None)
    return jax.shard_map(body, mesh=fine, in_specs=in_specs, out_specs=out_specs, check_vma=False)
```

```python
import jax
import jax.numpy as jnp
from jax import lax
from jax.experimental import pallas as pl
from jax.experimental.pallas import tpu as pltpu
from jax.sharding import Mesh, PartitionSpec as P

HEADS = 8
SHEADS = 4
HD = 128
MAXNB = 4
BLK = 128
NB = 4
CLIP = 8
EPS = 1e-06
NEG = -jnp.inf
LOG2E = 1.4426950408889634
F32 = jnp.float32
BF16 = jnp.bfloat16


def dot(a, b):
    return jnp.dot(a, b, preferred_element_type=F32)


def dot_t(a, b):
    return lax.dot_general(a, b, (((1,), (1,)), ((), ())), preferred_element_type=F32)


def modulate(rows, shift, gain):
    mean = jnp.mean(rows, axis=-1, keepdims=True)
    centred = rows - mean
    var = jnp.mean(centred * centred, axis=-1, keepdims=True)
    return (centred * lax.rsqrt(var + EPS) * gain + shift).astype(BF16)


def one_hot_rows(slot_row):
    tokens = slot_row.shape[1]
    cols = jnp.broadcast_to(slot_row, (128, tokens)).T
    lane = lax.broadcasted_iota(jnp.int32, (tokens, 128), 1)
    parts = [
        (cols == lane + 128 * c).astype(F32).astype(BF16) for c in range(tokens // 128)
    ]
    return jnp.concatenate(parts, axis=1)


def spatial_keyval(x_hbm, cond_hbm, slot_hbm, w_hbm, kv_hbm, mod_hbm, cond_ref, slot_ref, x_s, w_s, mod_s, kv_s, sem):
    tokens, width = x_s.shape
    half = width // 2
    x_in = pltpu.make_async_copy(x_hbm.at[0], x_s, sem.at[7])
    s_in = pltpu.make_async_copy(slot_hbm, slot_ref, sem.at[8])
    c_in = pltpu.make_async_copy(cond_hbm, cond_ref, sem.at[9])
    s_in.start()
    x_in.start()
    c_in.start()
    s_in.wait()
    perm = one_hot_rows(slot_ref[...])
    x_in.wait()
    c_in.wait()
    shift = cond_ref[0:1, :]
    gain = 1.0 + cond_ref[1:2, :]
    w_in = []
    for i in range(2):
        cs = slice(i * half, (i + 1) * half)
        copy = pltpu.make_async_copy(w_hbm.at[:, pl.ds((i + 1) * width, half)], w_s.at[:, cs], sem.at[i])
        copy.start()
        w_in.append(copy)
    for j in range(NB):
        sl = slice(j * BLK, (j + 1) * BLK)
        mod_s[sl, :] = modulate(dot(perm[sl, :], x_s[...]), shift, gain)
    outs = [pltpu.make_async_copy(mod_s, mod_hbm, sem.at[2])]
    outs[0].start()
    quarter = half // 2
    for i in range(4):
        if i % 2 == 0:
            w_in[i // 2].wait()
        cs = slice(i * quarter, (i + 1) * quarter)
        kv_s[:, cs] = dot(mod_s[...], w_s[:, cs]).astype(BF16)
        out = pltpu.make_async_copy(kv_s.at[:, cs], kv_hbm.at[:, cs], sem.at[3 + i])
        out.start()
        outs.append(out)
    for out in outs:
        out.wait()


def spatial_query(mod_hbm, w_hbm, q_ref, mod_s, w_s, sem):
    half = q_ref.shape[1]
    w_in = pltpu.make_async_copy(w_hbm.at[:, pl.ds(0, half)], w_s, sem.at[0])
    m_in = pltpu.make_async_copy(mod_hbm, mod_s, sem.at[1])
    w_in.start()
    m_in.start()
    w_in.wait()
    m_in.wait()
    q_ref[...] = dot(mod_s[...], w_s[...]).astype(BF16)


def temporal(x_ref, cond_hbm, w_hbm, o_hbm, cond_ref, w_s, mod_s, p_s, o_s, sem):
    frames, count, width = x_ref.shape
    half = width // 2
    c_in = pltpu.make_async_copy(cond_hbm, cond_ref, sem.at[7])
    c_in.start()
    w_in = []
    for i in range(3):
        copy = pltpu.make_async_copy(
            w_hbm.at[:, pl.ds(i * width + half, half)], w_s.at[:, pl.ds(i * half, half)], sem.at[i]
        )
        copy.start()
        w_in.append(copy)
    c_in.wait()
    shift = cond_ref[0:1, :]
    gain = 1.0 + cond_ref[1:2, :]
    for f in range(0, frames, 2):
        piece = x_ref[f : f + 2].reshape(2 * count, width).astype(F32)
        mod_s[f * count : (f + 2) * count, :] = modulate(piece, shift, gain)
    for i in range(3):
        w_in[i].wait()
        cs = slice(i * half, (i + 1) * half)
        p_s[:, :, cs] = dot(mod_s[...], w_s[:, cs]).astype(BF16).reshape(frames, count, half)
    group = 128 // frames
    scale = 1.0 / jnp.sqrt(F32(HD))
    ri = lax.broadcasted_iota(jnp.int32, (128, 128), 0) % group
    ci = lax.broadcasted_iota(jnp.int32, (128, 128), 1) % group
    same = ri == ci
    outs = []
    for t in range(count // group):
        ts = slice(t * group, (t + 1) * group)

        def part(i, h):
            lo = i * half + h * HD
            return p_s[:, ts, lo : lo + HD].reshape(128, HD)

        heads = range(SHEADS)
        ss = [jnp.where(same, dot_t(part(0, h), part(1, h)) * scale, NEG) for h in heads]
        es = [jnp.exp(s - jnp.max(s, axis=-1, keepdims=True)) for s in ss]
        ws = [e * (1.0 / jnp.sum(e, axis=-1, keepdims=True)) for e in es]
        his = [w.astype(BF16) for w in ws]
        los = [(w - hi.astype(F32)).astype(BF16) for w, hi in zip(ws, his)]
        for h in heads:
            o = dot(his[h], part(2, h)) + dot(los[h], part(2, h))
            o_s[:, ts, h * HD : (h + 1) * HD] = o.astype(BF16).reshape(frames, group, HD)
        out = pltpu.make_async_copy(o_s.at[:, ts], o_hbm.at[:, ts], sem.at[3 + t])
        out.start()
        outs.append(out)
    for out in outs:
        out.wait()


def finish(nb_hbm, cnt_hbm, x_hbm, cond_hbm, slot_hbm, q_hbm, kv_hbm, left_hbm, right_hbm, t_ref, w_ref, o_hbm,
           nb_ref, cnt_ref, cond_ref, slot_ref, x_s, q_ref, win, blk_s, acc_s, o_s, sem):
    tokens, width = x_s.shape
    half = width // 2
    copies = [
        (left_hbm, win.at[pl.ds(0, tokens)]),
        (right_hbm, win.at[pl.ds(2 * tokens, tokens)]),
        (kv_hbm, win.at[pl.ds(tokens, tokens)]),
        (q_hbm, q_ref),
        (slot_hbm, slot_ref),
        (nb_hbm, nb_ref),
        (cnt_hbm, cnt_ref),
        (cond_hbm, cond_ref),
        (x_hbm.at[0], x_s),
    ]
    copies = [pltpu.make_async_copy(a, b, sem.at[i]) for i, (a, b) in enumerate(copies)]
    for c in copies[4:8] + copies[:4]:
        c.start()
    acc_s[...] = dot(t_ref[...], w_ref[half:, :])
    copies[4].wait()
    tok = lax.broadcasted_iota(jnp.int32, (tokens, tokens), 0)
    unperm = (tok == slot_ref[...]).astype(F32).astype(BF16)
    scale = 1.0 / jnp.sqrt(F32(HD))
    total = 12 * NB
    for c in copies[:4] + copies[5:8]:
        c.wait()
    first = nb_ref[0, 0]
    copies[8].start()

    def select(j):
        starts = []
        lane = lax.broadcasted_iota(jnp.int32, (BLK, MAXNB * BLK), 1)
        keep = lane < cnt_ref[j] * BLK
        for n in range(MAXNB):
            at = lax.rem(nb_ref[j, n] - first + NB + total, total)
            at = jnp.minimum(at, 3 * NB - 1)
            starts.append(pl.multiple_of(at * BLK, BLK))

        def listed(lo):
            return jnp.concatenate([win[pl.ds(at, BLK), lo : lo + HD] for at in starts], axis=0)

        return slice(j * BLK, (j + 1) * BLK), keep, listed

    def score(item):
        (rows, keep, listed), h = item
        return jnp.where(keep, dot_t(q_ref[rows, h * HD : (h + 1) * HD], listed(h * HD)), NEG)

    items = [(sel, h) for sel in map(select, range(NB)) for h in range(SHEADS)]
    step = 2
    now = [score(item) for item in items[:step]]
    for g in range(0, len(items), step):
        ahead = [score(item) for item in items[g + step : g + 2 * step]]
        tops = [jnp.max(s, axis=-1, keepdims=True) for s in now]
        es = [jnp.exp2((s - top) * (scale * LOG2E)) for s, top in zip(now, tops)]
        invs = [1.0 / jnp.sum(e, axis=-1, keepdims=True) for e in es]
        for ((rows, _, listed), h), e, inv in zip(items[g : g + step], es, invs):
            o = dot(e.astype(BF16), listed(half + h * HD)) * inv
            blk_s[rows, h * HD : (h + 1) * HD] = o.astype(BF16)
        now = ahead
    copies[8].wait()
    gate = cond_ref[2:3, :]
    outs = []
    sp = dot(unperm, blk_s[...]).astype(BF16)
    quarter = width // 4
    for i in range(4):
        cs = slice(i * quarter, (i + 1) * quarter)
        mixed = dot(sp, w_ref[:half, cs]) + acc_s[:, cs]
        o_s[:, cs] = (x_s[:, cs].astype(F32) + gate[:, cs] * mixed).astype(BF16)
        out = pltpu.make_async_copy(o_s.at[:, cs], o_hbm.at[0, :, cs], sem.at[9 + i])
        out.start()
        outs.append(out)
    for out in outs:
        out.wait()


HB = pl.BlockSpec(memory_space=pltpu.HBM)
VM = pl.BlockSpec(memory_space=pltpu.VMEM)
DMA = pltpu.SemaphoreType.DMA


def near(x):
    return pltpu.with_memory_space_constraint(x, pltpu.VMEM)


def call(kernel, ins, outs, shapes, scratch):
    return pl.pallas_call(
        kernel,
        out_shape=shapes,
        in_specs=ins,
        out_specs=outs,
        scratch_shapes=scratch,
        name=kernel.__name__,
    )


def body(latent, cond, w_qkv, w_out, slot, neighbours, counts):
    tokens, width = latent.shape[1], latent.shape[2]
    half = width // 2
    per = tokens // CLIP
    slot_row = slot.reshape(1, tokens)
    arr = jax.ShapeDtypeStruct
    room = lambda *shape: pltpu.VMEM(shape, BF16)
    seen = lax.all_to_all(latent.reshape(CLIP, per, width), "member", 0, 0, tiled=True)
    kv, mod = call(
        spatial_keyval,
        [HB, HB, HB, HB],
        (HB, HB),
        (arr((tokens, width), BF16), arr((tokens, width), BF16)),
        [
            pltpu.VMEM((3, width), F32),
            pltpu.VMEM((1, tokens), jnp.int32),
            room(tokens, width),
            room(width, width),
            room(tokens, width),
            room(tokens, width),
            DMA((10,)),
        ],
    )(latent, cond, slot_row, w_qkv)
    count = lax.axis_size("space")
    left = lax.ppermute(kv, "space", [(i, (i + 1) % count) for i in range(count)])
    right = lax.ppermute(kv, "space", [((i + 1) % count, i) for i in range(count)])
    q = call(
        spatial_query,
        [HB, HB],
        VM,
        arr((tokens, half), BF16),
        [room(tokens, width), room(width, half), DMA((2,))],
    )(mod, w_qkv)
    t_out = call(
        temporal,
        [VM, HB, HB],
        HB,
        arr((CLIP, per, half), BF16),
        [
            pltpu.VMEM((3, width), F32),
            room(width, 3 * half),
            room(tokens, width),
            room(CLIP, per, 3 * half),
            room(CLIP, per, half),
            DMA((8,)),
        ],
    )(near(seen), cond, w_qkv)
    back = lax.all_to_all(t_out, "member", 0, 0, tiled=True).reshape(tokens, half)
    return call(
        finish,
        [HB] * 9 + [VM, VM],
        HB,
        arr((1, tokens, width), BF16),
        [
            pltpu.SMEM((NB, MAXNB), jnp.int32),
            pltpu.SMEM((NB,), jnp.int32),
            pltpu.VMEM((3, width), F32),
            pltpu.VMEM((1, tokens), jnp.int32),
            room(tokens, width),
            room(tokens, half),
            room(3 * tokens, width),
            room(tokens, half),
            pltpu.VMEM((tokens, width), F32),
            room(tokens, width),
            DMA((13,)),
        ],
    )(neighbours, counts, latent, cond, slot_row, q, kv, left, right, near(back), near(w_out))


def solution(mesh):
    devices = mesh.devices
    spaces, frames = devices.shape
    fine = Mesh(devices.reshape(spaces, frames // CLIP, CLIP), ("space", "clip", "member"))
    whole = ("clip", "member")
    in_specs = (P(whole, "space", None), P(), P(), P(), P("space"), P("space", None), P("space"))
    out_specs = P(whole, "space", None)
    return jax.shard_map(body, mesh=fine, in_specs=in_specs, out_specs=out_specs, check_vma=False)
```

```python
import jax
import jax.numpy as jnp
from jax import lax
from jax.experimental import pallas as pl
from jax.experimental.pallas import tpu as pltpu
from jax.sharding import Mesh, PartitionSpec as P

HEADS = 8
SHEADS = 4
HD = 128
MAXNB = 4
BLK = 128
NB = 4
CLIP = 8
EPS = 1e-06
NEG = -jnp.inf
LOG2E = 1.4426950408889634
F32 = jnp.float32
BF16 = jnp.bfloat16


def dot(a, b):
    return jnp.dot(a, b, preferred_element_type=F32)


def dot_t(a, b):
    return lax.dot_general(a, b, (((1,), (1,)), ((), ())), preferred_element_type=F32)


def modulate(rows, shift, gain):
    mean = jnp.mean(rows, axis=-1, keepdims=True)
    centred = rows - mean
    var = jnp.mean(centred * centred, axis=-1, keepdims=True)
    return (centred * lax.rsqrt(var + EPS) * gain + shift).astype(BF16)


def one_hot_rows(slot_row):
    tokens = slot_row.shape[1]
    cols = jnp.broadcast_to(slot_row, (128, tokens)).T
    lane = lax.broadcasted_iota(jnp.int32, (tokens, 128), 1)
    parts = [
        (cols == lane + 128 * c).astype(F32).astype(BF16) for c in range(tokens // 128)
    ]
    return jnp.concatenate(parts, axis=1)


def spatial_keyval(x_hbm, cond_hbm, slot_hbm, w_hbm, kv_hbm, mod_hbm, cond_ref, slot_ref, x_s, w_s, mod_s, kv_s, sem):
    tokens, width = x_s.shape
    half = width // 2
    x_in = pltpu.make_async_copy(x_hbm.at[0], x_s, sem.at[7])
    s_in = pltpu.make_async_copy(slot_hbm, slot_ref, sem.at[8])
    c_in = pltpu.make_async_copy(cond_hbm, cond_ref, sem.at[9])
    s_in.start()
    x_in.start()
    c_in.start()
    s_in.wait()
    perm = one_hot_rows(slot_ref[...])
    x_in.wait()
    c_in.wait()
    shift = cond_ref[0:1, :]
    gain = 1.0 + cond_ref[1:2, :]
    w_in = []
    for i in range(2):
        cs = slice(i * half, (i + 1) * half)
        copy = pltpu.make_async_copy(w_hbm.at[:, pl.ds((i + 1) * width, half)], w_s.at[:, cs], sem.at[i])
        copy.start()
        w_in.append(copy)
    for j in range(NB):
        sl = slice(j * BLK, (j + 1) * BLK)
        mod_s[sl, :] = modulate(dot(perm[sl, :], x_s[...]), shift, gain)
    outs = [pltpu.make_async_copy(mod_s, mod_hbm, sem.at[2])]
    outs[0].start()
    quarter = half // 2
    for i in range(4):
        if i % 2 == 0:
            w_in[i // 2].wait()
        cs = slice(i * quarter, (i + 1) * quarter)
        kv_s[:, cs] = dot(mod_s[...], w_s[:, cs]).astype(BF16)
        out = pltpu.make_async_copy(kv_s.at[:, cs], kv_hbm.at[:, cs], sem.at[3 + i])
        out.start()
        outs.append(out)
    for out in outs:
        out.wait()


def spatial_query(mod_hbm, w_hbm, q_ref, mod_s, w_s, sem):
    half = q_ref.shape[1]
    w_in = pltpu.make_async_copy(w_hbm.at[:, pl.ds(0, half)], w_s, sem.at[0])
    m_in = pltpu.make_async_copy(mod_hbm, mod_s, sem.at[1])
    w_in.start()
    m_in.start()
    w_in.wait()
    m_in.wait()
    q_ref[...] = dot(mod_s[...], w_s[...]).astype(BF16)


def temporal(x_ref, cond_hbm, w_hbm, o_hbm, cond_ref, w_s, mod_s, p_s, o_s, sem):
    frames, count, width = x_ref.shape
    half = width // 2
    c_in = pltpu.make_async_copy(cond_hbm, cond_ref, sem.at[7])
    c_in.start()
    w_in = []
    for i in range(3):
        copy = pltpu.make_async_copy(
            w_hbm.at[:, pl.ds(i * width + half, half)], w_s.at[:, pl.ds(i * half, half)], sem.at[i]
        )
        copy.start()
        w_in.append(copy)
    c_in.wait()
    shift = cond_ref[0:1, :]
    gain = 1.0 + cond_ref[1:2, :]
    for f in range(0, frames, 2):
        piece = x_ref[f : f + 2].reshape(2 * count, width).astype(F32)
        mod_s[f * count : (f + 2) * count, :] = modulate(piece, shift, gain)
    for i in range(3):
        w_in[i].wait()
        cs = slice(i * half, (i + 1) * half)
        p_s[:, :, cs] = dot(mod_s[...], w_s[:, cs]).astype(BF16).reshape(frames, count, half)
    group = 128 // frames
    scale = 1.0 / jnp.sqrt(F32(HD))
    ri = lax.broadcasted_iota(jnp.int32, (128, 128), 0) % group
    ci = lax.broadcasted_iota(jnp.int32, (128, 128), 1) % group
    same = ri == ci
    outs = []
    for t in range(count // group):
        ts = slice(t * group, (t + 1) * group)

        def part(i, h):
            lo = i * half + h * HD
            return p_s[:, ts, lo : lo + HD].reshape(128, HD)

        heads = range(SHEADS)
        ss = [jnp.where(same, dot_t(part(0, h), part(1, h)) * scale, NEG) for h in heads]
        es = [jnp.exp(s - jnp.max(s, axis=-1, keepdims=True)) for s in ss]
        ws = [e * (1.0 / jnp.sum(e, axis=-1, keepdims=True)) for e in es]
        his = [w.astype(BF16) for w in ws]
        los = [(w - hi.astype(F32)).astype(BF16) for w, hi in zip(ws, his)]
        for h in heads:
            o = dot(his[h], part(2, h)) + dot(los[h], part(2, h))
            o_s[:, ts, h * HD : (h + 1) * HD] = o.astype(BF16).reshape(frames, group, HD)
        out = pltpu.make_async_copy(o_s.at[:, ts], o_hbm.at[:, ts], sem.at[3 + t])
        out.start()
        outs.append(out)
    for out in outs:
        out.wait()


def temporal_out(t_ref, w_hbm, x_hbm, cond_hbm, o_ref, w_s, x_s, cond_ref, sem):
    half = t_ref.shape[1]
    copies = [
        (w_hbm.at[pl.ds(half, half)], w_s),
        (x_hbm.at[0], x_s),
        (cond_hbm, cond_ref),
    ]
    copies = [pltpu.make_async_copy(a, b, sem.at[i]) for i, (a, b) in enumerate(copies)]
    for c in copies:
        c.start()
    for c in copies:
        c.wait()
    o_ref[...] = x_s[...].astype(F32) + cond_ref[2:3, :] * dot(t_ref[...], w_s[...])


def finish(nb_hbm, cnt_hbm, acc_hbm, cond_hbm, slot_hbm, q_hbm, kv_hbm, left_ref, right_ref, w_hbm, o_hbm,
           nb_ref, cnt_ref, cond_ref, slot_ref, q_ref, win, blk_s, acc_s, w_s, o_s, sem):
    tokens, width = acc_s.shape
    half = width // 2
    copies = [
        (slot_hbm, slot_ref),
        (nb_hbm, nb_ref),
        (cnt_hbm, cnt_ref),
        (q_hbm, q_ref),
        (kv_hbm, win.at[pl.ds(tokens, tokens)]),
        (cond_hbm, cond_ref),
        (w_hbm.at[pl.ds(0, half)], w_s),
        (acc_hbm, acc_s),
    ]
    copies = [pltpu.make_async_copy(a, b, sem.at[i]) for i, (a, b) in enumerate(copies)]
    for c in copies[:6]:
        c.start()
    win[:tokens, :] = left_ref[...]
    win[2 * tokens :, :] = right_ref[...]
    copies[0].wait()
    tok = lax.broadcasted_iota(jnp.int32, (tokens, tokens), 0)
    unperm = (tok == slot_ref[...]).astype(F32).astype(BF16)
    scale = 1.0 / jnp.sqrt(F32(HD))
    total = 12 * NB
    for c in copies[1:6]:
        c.wait()
    for c in copies[6:]:
        c.start()
    first = nb_ref[0, 0]

    def select(j):
        starts = []
        lane = lax.broadcasted_iota(jnp.int32, (BLK, MAXNB * BLK), 1)
        keep = lane < cnt_ref[j] * BLK
        for n in range(MAXNB):
            at = lax.rem(nb_ref[j, n] - first + NB + total, total)
            at = jnp.minimum(at, 3 * NB - 1)
            starts.append(pl.multiple_of(at * BLK, BLK))

        def listed(lo):
            return jnp.concatenate([win[pl.ds(at, BLK), lo : lo + HD] for at in starts], axis=0)

        return slice(j * BLK, (j + 1) * BLK), keep, listed

    def score(item):
        (rows, keep, listed), h = item
        return jnp.where(keep, dot_t(q_ref[rows, h * HD : (h + 1) * HD], listed(h * HD)), NEG)

    items = [(sel, h) for sel in map(select, range(NB)) for h in range(SHEADS)]
    step = 2
    now = [score(item) for item in items[:step]]
    for g in range(0, len(items), step):
        ahead = [score(item) for item in items[g + step : g + 2 * step]]
        tops = [jnp.max(s, axis=-1, keepdims=True) for s in now]
        es = [jnp.exp2((s - top) * (scale * LOG2E)) for s, top in zip(now, tops)]
        invs = [1.0 / jnp.sum(e, axis=-1, keepdims=True) for e in es]
        for ((rows, _, listed), h), e, inv in zip(items[g : g + step], es, invs):
            o = dot(e.astype(BF16), listed(half + h * HD)) * inv
            blk_s[rows, h * HD : (h + 1) * HD] = o.astype(BF16)
        now = ahead
    copies[6].wait()
    copies[7].wait()
    gate = cond_ref[2:3, :]
    outs = []
    sp = dot(unperm, blk_s[...]).astype(BF16)
    quarter = width // 4
    for i in range(4):
        cs = slice(i * quarter, (i + 1) * quarter)
        o_s[:, cs] = (acc_s[:, cs] + gate[:, cs] * dot(sp, w_s[:, cs])).astype(BF16)
        out = pltpu.make_async_copy(o_s.at[:, cs], o_hbm.at[0, :, cs], sem.at[8 + i])
        out.start()
        outs.append(out)
    for out in outs:
        out.wait()


HB = pl.BlockSpec(memory_space=pltpu.HBM)
VM = pl.BlockSpec(memory_space=pltpu.VMEM)
DMA = pltpu.SemaphoreType.DMA


def near(x):
    return pltpu.with_memory_space_constraint(x, pltpu.VMEM)


def call(kernel, ins, outs, shapes, scratch):
    return pl.pallas_call(
        kernel,
        out_shape=shapes,
        in_specs=ins,
        out_specs=outs,
        scratch_shapes=scratch,
        name=kernel.__name__,
    )


def body(latent, cond, w_qkv, w_out, slot, neighbours, counts):
    tokens, width = latent.shape[1], latent.shape[2]
    half = width // 2
    per = tokens // CLIP
    slot_row = slot.reshape(1, tokens)
    arr = jax.ShapeDtypeStruct
    room = lambda *shape: pltpu.VMEM(shape, BF16)
    seen = lax.all_to_all(latent.reshape(CLIP, per, width), "member", 0, 0, tiled=True)
    kv, mod = call(
        spatial_keyval,
        [HB, HB, HB, HB],
        (HB, HB),
        (arr((tokens, width), BF16), arr((tokens, width), BF16)),
        [
            pltpu.VMEM((3, width), F32),
            pltpu.VMEM((1, tokens), jnp.int32),
            room(tokens, width),
            room(width, width),
            room(tokens, width),
            room(tokens, width),
            DMA((10,)),
        ],
    )(latent, cond, slot_row, w_qkv)
    count = lax.axis_size("space")
    left = lax.ppermute(kv, "space", [(i, (i + 1) % count) for i in range(count)])
    right = lax.ppermute(kv, "space", [((i + 1) % count, i) for i in range(count)])
    q = call(
        spatial_query,
        [HB, HB],
        VM,
        arr((tokens, half), BF16),
        [room(tokens, width), room(width, half), DMA((2,))],
    )(mod, w_qkv)
    t_out = call(
        temporal,
        [VM, HB, HB],
        HB,
        arr((CLIP, per, half), BF16),
        [
            pltpu.VMEM((3, width), F32),
            room(width, 3 * half),
            room(tokens, width),
            room(CLIP, per, 3 * half),
            room(CLIP, per, half),
            DMA((8,)),
        ],
    )(near(seen), cond, w_qkv)
    back = lax.all_to_all(t_out, "member", 0, 0, tiled=True).reshape(tokens, half)
    acc = call(
        temporal_out,
        [VM, HB, HB, HB],
        VM,
        arr((tokens, width), F32),
        [room(half, width), room(tokens, width), pltpu.VMEM((3, width), F32), DMA((3,))],
    )(near(back), w_out, latent, cond)
    return call(
        finish,
        [HB] * 7 + [VM, VM, HB],
        HB,
        arr((1, tokens, width), BF16),
        [
            pltpu.SMEM((NB, MAXNB), jnp.int32),
            pltpu.SMEM((NB,), jnp.int32),
            pltpu.VMEM((3, width), F32),
            pltpu.VMEM((1, tokens), jnp.int32),
            room(tokens, half),
            room(3 * tokens, width),
            room(tokens, half),
            pltpu.VMEM((tokens, width), F32),
            room(half, width),
            room(tokens, width),
            DMA((12,)),
        ],
    )(neighbours, counts, acc, cond, slot_row, q, kv, near(left), near(right), w_out)


def solution(mesh):
    devices = mesh.devices
    spaces, frames = devices.shape
    fine = Mesh(devices.reshape(spaces, frames // CLIP, CLIP), ("space", "clip", "member"))
    whole = ("clip", "member")
    in_specs = (P(whole, "space", None), P(), P(), P(), P("space"), P("space", None), P("space"))
    out_specs = P(whole, "space", None)
    return jax.shard_map(body, mesh=fine, in_specs=in_specs, out_specs=out_specs, check_vma=False)
```

```python
import jax
import jax.numpy as jnp
from jax import lax
from jax.experimental import pallas as pl
from jax.experimental.pallas import tpu as pltpu
from jax.sharding import Mesh, PartitionSpec as P

HEADS = 8
SHEADS = 4
HD = 128
MAXNB = 4
BLK = 128
NB = 4
CLIP = 8
EPS = 1e-06
NEG = -jnp.inf
LOG2E = 1.4426950408889634
F32 = jnp.float32
BF16 = jnp.bfloat16


def dot(a, b):
    return jnp.dot(a, b, preferred_element_type=F32)


def dot_t(a, b):
    return lax.dot_general(a, b, (((1,), (1,)), ((), ())), preferred_element_type=F32)


def modulate(rows, shift, gain):
    mean = jnp.mean(rows, axis=-1, keepdims=True)
    centred = rows - mean
    var = jnp.mean(centred * centred, axis=-1, keepdims=True)
    return (centred * lax.rsqrt(var + EPS) * gain + shift).astype(BF16)


def one_hot_rows(slot_row):
    tokens = slot_row.shape[1]
    cols = jnp.broadcast_to(slot_row, (128, tokens)).T
    lane = lax.broadcasted_iota(jnp.int32, (tokens, 128), 1)
    parts = [
        (cols == lane + 128 * c).astype(F32).astype(BF16) for c in range(tokens // 128)
    ]
    return jnp.concatenate(parts, axis=1)


def spatial_keyval(x_hbm, cond_hbm, slot_hbm, w_hbm, kv_hbm, mod_hbm, cond_ref, slot_ref, x_s, w_s, mod_s, kv_s, sem):
    tokens, width = x_s.shape
    half = width // 2
    x_in = pltpu.make_async_copy(x_hbm.at[0], x_s, sem.at[7])
    s_in = pltpu.make_async_copy(slot_hbm, slot_ref, sem.at[8])
    c_in = pltpu.make_async_copy(cond_hbm, cond_ref, sem.at[9])
    s_in.start()
    x_in.start()
    c_in.start()
    s_in.wait()
    perm = one_hot_rows(slot_ref[...])
    x_in.wait()
    c_in.wait()
    shift = cond_ref[0:1, :]
    gain = 1.0 + cond_ref[1:2, :]
    w_in = []
    for i in range(2):
        cs = slice(i * half, (i + 1) * half)
        copy = pltpu.make_async_copy(w_hbm.at[:, pl.ds((i + 1) * width, half)], w_s.at[:, cs], sem.at[i])
        copy.start()
        w_in.append(copy)
    for j in range(NB):
        sl = slice(j * BLK, (j + 1) * BLK)
        mod_s[sl, :] = modulate(dot(perm[sl, :], x_s[...]), shift, gain)
    outs = [pltpu.make_async_copy(mod_s, mod_hbm, sem.at[2])]
    outs[0].start()
    quarter = half // 2
    for i in range(4):
        if i % 2 == 0:
            w_in[i // 2].wait()
        cs = slice(i * quarter, (i + 1) * quarter)
        kv_s[:, cs] = dot(mod_s[...], w_s[:, cs]).astype(BF16)
        out = pltpu.make_async_copy(kv_s.at[:, cs], kv_hbm.at[:, cs], sem.at[3 + i])
        out.start()
        outs.append(out)
    for out in outs:
        out.wait()


def spatial_query(mod_hbm, w_hbm, q_ref, mod_s, w_s, sem):
    half = q_ref.shape[1]
    w_in = pltpu.make_async_copy(w_hbm.at[:, pl.ds(0, half)], w_s, sem.at[0])
    m_in = pltpu.make_async_copy(mod_hbm, mod_s, sem.at[1])
    w_in.start()
    m_in.start()
    w_in.wait()
    m_in.wait()
    q_ref[...] = dot(mod_s[...], w_s[...]).astype(BF16)


def temporal(x_ref, cond_hbm, w_hbm, o_hbm, cond_ref, w_s, mod_s, p_s, o_s, sem):
    frames, count, width = x_ref.shape
    half = width // 2
    c_in = pltpu.make_async_copy(cond_hbm, cond_ref, sem.at[7])
    c_in.start()
    w_in = []
    for i in range(3):
        copy = pltpu.make_async_copy(
            w_hbm.at[:, pl.ds(i * width + half, half)], w_s.at[:, pl.ds(i * half, half)], sem.at[i]
        )
        copy.start()
        w_in.append(copy)
    c_in.wait()
    shift = cond_ref[0:1, :]
    gain = 1.0 + cond_ref[1:2, :]
    for f in range(0, frames, 2):
        piece = x_ref[f : f + 2].reshape(2 * count, width).astype(F32)
        mod_s[f * count : (f + 2) * count, :] = modulate(piece, shift, gain)
    for i in range(3):
        w_in[i].wait()
        cs = slice(i * half, (i + 1) * half)
        p_s[:, :, cs] = dot(mod_s[...], w_s[:, cs]).astype(BF16).reshape(frames, count, half)
    group = 128 // frames
    scale = 1.0 / jnp.sqrt(F32(HD))
    ri = lax.broadcasted_iota(jnp.int32, (128, 128), 0) % group
    ci = lax.broadcasted_iota(jnp.int32, (128, 128), 1) % group
    same = ri == ci
    outs = []
    for t in range(count // group):
        ts = slice(t * group, (t + 1) * group)

        def part(i, h):
            lo = i * half + h * HD
            return p_s[:, ts, lo : lo + HD].reshape(128, HD)

        heads = range(SHEADS)
        ss = [jnp.where(same, dot_t(part(0, h), part(1, h)) * scale, NEG) for h in heads]
        es = [jnp.exp(s - jnp.max(s, axis=-1, keepdims=True)) for s in ss]
        ws = [e * (1.0 / jnp.sum(e, axis=-1, keepdims=True)) for e in es]
        his = [w.astype(BF16) for w in ws]
        los = [(w - hi.astype(F32)).astype(BF16) for w, hi in zip(ws, his)]
        for h in heads:
            o = dot(his[h], part(2, h)) + dot(los[h], part(2, h))
            o_s[:, ts, h * HD : (h + 1) * HD] = o.astype(BF16).reshape(frames, group, HD)
        out = pltpu.make_async_copy(o_s.at[:, ts], o_hbm.at[:, ts], sem.at[3 + t])
        out.start()
        outs.append(out)
    for out in outs:
        out.wait()


def temporal_out(t_hbm, w_hbm, x_hbm, cond_hbm, o_ref, t_s, w_s, x_s, cond_ref, sem):
    tokens, half = t_s.shape
    copies = [
        (t_hbm, t_s),
        (w_hbm.at[pl.ds(half, half)], w_s),
        (x_hbm.at[0], x_s),
        (cond_hbm, cond_ref),
    ]
    copies = [pltpu.make_async_copy(a, b, sem.at[i]) for i, (a, b) in enumerate(copies)]
    for c in copies:
        c.start()
    for c in copies:
        c.wait()
    o_ref[...] = x_s[...].astype(F32) + cond_ref[2:3, :] * dot(t_s[...], w_s[...])


def finish(nb_hbm, cnt_hbm, acc_hbm, cond_hbm, slot_hbm, q_hbm, kv_hbm, left_ref, right_ref, w_hbm, o_hbm,
           nb_ref, cnt_ref, cond_ref, slot_ref, q_ref, win, blk_s, acc_s, w_s, o_s, sem):
    tokens, width = acc_s.shape
    half = width // 2
    copies = [
        (slot_hbm, slot_ref),
        (nb_hbm, nb_ref),
        (cnt_hbm, cnt_ref),
        (q_hbm, q_ref),
        (kv_hbm, win.at[pl.ds(tokens, tokens)]),
        (cond_hbm, cond_ref),
        (w_hbm.at[pl.ds(0, half)], w_s),
        (acc_hbm, acc_s),
    ]
    copies = [pltpu.make_async_copy(a, b, sem.at[i]) for i, (a, b) in enumerate(copies)]
    for c in copies[:6]:
        c.start()
    win[:tokens, :] = left_ref[...]
    win[2 * tokens :, :] = right_ref[...]
    copies[0].wait()
    tok = lax.broadcasted_iota(jnp.int32, (tokens, tokens), 0)
    unperm = (tok == slot_ref[...]).astype(F32).astype(BF16)
    scale = 1.0 / jnp.sqrt(F32(HD))
    total = 12 * NB
    for c in copies[1:6]:
        c.wait()
    for c in copies[6:]:
        c.start()
    first = nb_ref[0, 0]

    def select(j):
        starts = []
        lane = lax.broadcasted_iota(jnp.int32, (BLK, MAXNB * BLK), 1)
        keep = lane < cnt_ref[j] * BLK
        for n in range(MAXNB):
            at = lax.rem(nb_ref[j, n] - first + NB + total, total)
            at = jnp.minimum(at, 3 * NB - 1)
            starts.append(pl.multiple_of(at * BLK, BLK))

        def listed(lo):
            return jnp.concatenate([win[pl.ds(at, BLK), lo : lo + HD] for at in starts], axis=0)

        return slice(j * BLK, (j + 1) * BLK), keep, listed

    def score(item):
        (rows, keep, listed), h = item
        return jnp.where(keep, dot_t(q_ref[rows, h * HD : (h + 1) * HD], listed(h * HD)), NEG)

    items = [(sel, h) for sel in map(select, range(NB)) for h in range(SHEADS)]
    step = 2
    now = [score(item) for item in items[:step]]
    for g in range(0, len(items), step):
        ahead = [score(item) for item in items[g + step : g + 2 * step]]
        tops = [jnp.max(s, axis=-1, keepdims=True) for s in now]
        es = [jnp.exp2((s - top) * (scale * LOG2E)) for s, top in zip(now, tops)]
        invs = [1.0 / jnp.sum(e, axis=-1, keepdims=True) for e in es]
        for ((rows, _, listed), h), e, inv in zip(items[g : g + step], es, invs):
            o = dot(e.astype(BF16), listed(half + h * HD)) * inv
            blk_s[rows, h * HD : (h + 1) * HD] = o.astype(BF16)
        now = ahead
    copies[6].wait()
    copies[7].wait()
    gate = cond_ref[2:3, :]
    outs = []
    sp = dot(unperm, blk_s[...]).astype(BF16)
    quarter = width // 4
    for i in range(4):
        cs = slice(i * quarter, (i + 1) * quarter)
        o_s[:, cs] = (acc_s[:, cs] + gate[:, cs] * dot(sp, w_s[:, cs])).astype(BF16)
        out = pltpu.make_async_copy(o_s.at[:, cs], o_hbm.at[0, :, cs], sem.at[8 + i])
        out.start()
        outs.append(out)
    for out in outs:
        out.wait()


HB = pl.BlockSpec(memory_space=pltpu.HBM)
VM = pl.BlockSpec(memory_space=pltpu.VMEM)
DMA = pltpu.SemaphoreType.DMA


def near(x):
    return pltpu.with_memory_space_constraint(x, pltpu.VMEM)


def call(kernel, ins, outs, shapes, scratch):
    return pl.pallas_call(
        kernel,
        out_shape=shapes,
        in_specs=ins,
        out_specs=outs,
        scratch_shapes=scratch,
        name=kernel.__name__,
    )


def body(latent, cond, w_qkv, w_out, slot, neighbours, counts):
    tokens, width = latent.shape[1], latent.shape[2]
    half = width // 2
    per = tokens // CLIP
    slot_row = slot.reshape(1, tokens)
    arr = jax.ShapeDtypeStruct
    room = lambda *shape: pltpu.VMEM(shape, BF16)
    seen = lax.all_to_all(latent.reshape(CLIP, per, width), "member", 0, 0, tiled=True)
    kv, mod = call(
        spatial_keyval,
        [HB, HB, HB, HB],
        (HB, HB),
        (arr((tokens, width), BF16), arr((tokens, width), BF16)),
        [
            pltpu.VMEM((3, width), F32),
            pltpu.VMEM((1, tokens), jnp.int32),
            room(tokens, width),
            room(width, width),
            room(tokens, width),
            room(tokens, width),
            DMA((10,)),
        ],
    )(latent, cond, slot_row, w_qkv)
    count = lax.axis_size("space")
    left = lax.ppermute(kv, "space", [(i, (i + 1) % count) for i in range(count)])
    right = lax.ppermute(kv, "space", [((i + 1) % count, i) for i in range(count)])
    q = call(
        spatial_query,
        [HB, HB],
        VM,
        arr((tokens, half), BF16),
        [room(tokens, width), room(width, half), DMA((2,))],
    )(mod, w_qkv)
    t_out = call(
        temporal,
        [VM, HB, HB],
        HB,
        arr((CLIP, per, half), BF16),
        [
            pltpu.VMEM((3, width), F32),
            room(width, 3 * half),
            room(tokens, width),
            room(CLIP, per, 3 * half),
            room(CLIP, per, half),
            DMA((8,)),
        ],
    )(near(seen), cond, w_qkv)
    back = lax.all_to_all(t_out, "member", 0, 0, tiled=True).reshape(tokens, half)
    acc = call(
        temporal_out,
        [HB, HB, HB, HB],
        VM,
        arr((tokens, width), F32),
        [room(tokens, half), room(half, width), room(tokens, width), pltpu.VMEM((3, width), F32), DMA((4,))],
    )(back, w_out, latent, cond)
    return call(
        finish,
        [HB] * 7 + [VM, VM, HB],
        HB,
        arr((1, tokens, width), BF16),
        [
            pltpu.SMEM((NB, MAXNB), jnp.int32),
            pltpu.SMEM((NB,), jnp.int32),
            pltpu.VMEM((3, width), F32),
            pltpu.VMEM((1, tokens), jnp.int32),
            room(tokens, half),
            room(3 * tokens, width),
            room(tokens, half),
            pltpu.VMEM((tokens, width), F32),
            room(half, width),
            room(tokens, width),
            DMA((12,)),
        ],
    )(neighbours, counts, acc, cond, slot_row, q, kv, near(left), near(right), w_out)


def solution(mesh):
    devices = mesh.devices
    spaces, frames = devices.shape
    fine = Mesh(devices.reshape(spaces, frames // CLIP, CLIP), ("space", "clip", "member"))
    whole = ("clip", "member")
    in_specs = (P(whole, "space", None), P(), P(), P(), P("space"), P("space", None), P("space"))
    out_specs = P(whole, "space", None)
    return jax.shard_map(body, mesh=fine, in_specs=in_specs, out_specs=out_specs, check_vma=False)
```

```python
import jax
import jax.numpy as jnp
from jax import lax
from jax.experimental import pallas as pl
from jax.experimental.pallas import tpu as pltpu
from jax.sharding import Mesh, PartitionSpec as P

HEADS = 8
SHEADS = 4
HD = 128
MAXNB = 4
BLK = 128
NB = 4
CLIP = 8
EPS = 1e-06
NEG = -jnp.inf
LOG2E = 1.4426950408889634
F32 = jnp.float32
BF16 = jnp.bfloat16


def dot(a, b):
    return jnp.dot(a, b, preferred_element_type=F32)


def dot_t(a, b):
    return lax.dot_general(a, b, (((1,), (1,)), ((), ())), preferred_element_type=F32)


def modulate(rows, shift, gain):
    mean = jnp.mean(rows, axis=-1, keepdims=True)
    centred = rows - mean
    var = jnp.mean(centred * centred, axis=-1, keepdims=True)
    return (centred * lax.rsqrt(var + EPS) * gain + shift).astype(BF16)


def one_hot_rows(slot_row):
    tokens = slot_row.shape[1]
    cols = jnp.broadcast_to(slot_row, (128, tokens)).T
    lane = lax.broadcasted_iota(jnp.int32, (tokens, 128), 1)
    parts = [
        (cols == lane + 128 * c).astype(F32).astype(BF16) for c in range(tokens // 128)
    ]
    return jnp.concatenate(parts, axis=1)


def spatial_keyval(x_hbm, cond_hbm, slot_hbm, w_hbm, kv_hbm, mod_hbm, cond_ref, slot_ref, x_s, w_s, mod_s, kv_s, sem):
    tokens, width = x_s.shape
    half = width // 2
    x_in = pltpu.make_async_copy(x_hbm.at[0], x_s, sem.at[7])
    s_in = pltpu.make_async_copy(slot_hbm, slot_ref, sem.at[8])
    c_in = pltpu.make_async_copy(cond_hbm, cond_ref, sem.at[9])
    s_in.start()
    x_in.start()
    c_in.start()
    s_in.wait()
    perm = one_hot_rows(slot_ref[...])
    x_in.wait()
    c_in.wait()
    shift = cond_ref[0:1, :]
    gain = 1.0 + cond_ref[1:2, :]
    w_in = []
    for i in range(2):
        cs = slice(i * half, (i + 1) * half)
        copy = pltpu.make_async_copy(w_hbm.at[:, pl.ds((i + 1) * width, half)], w_s.at[:, cs], sem.at[i])
        copy.start()
        w_in.append(copy)
    for j in range(NB):
        sl = slice(j * BLK, (j + 1) * BLK)
        mod_s[sl, :] = modulate(dot(perm[sl, :], x_s[...]), shift, gain)
    outs = [pltpu.make_async_copy(mod_s, mod_hbm, sem.at[2])]
    outs[0].start()
    quarter = half // 2
    for i in range(4):
        if i % 2 == 0:
            w_in[i // 2].wait()
        cs = slice(i * quarter, (i + 1) * quarter)
        kv_s[:, cs] = dot(mod_s[...], w_s[:, cs]).astype(BF16)
        out = pltpu.make_async_copy(kv_s.at[:, cs], kv_hbm.at[:, cs], sem.at[3 + i])
        out.start()
        outs.append(out)
    for out in outs:
        out.wait()


def spatial_query(mod_hbm, w_hbm, q_ref, mod_s, w_s, sem):
    half = q_ref.shape[1]
    w_in = pltpu.make_async_copy(w_hbm.at[:, pl.ds(0, half)], w_s, sem.at[0])
    m_in = pltpu.make_async_copy(mod_hbm, mod_s, sem.at[1])
    w_in.start()
    m_in.start()
    w_in.wait()
    m_in.wait()
    q_ref[...] = dot(mod_s[...], w_s[...]).astype(BF16)


def temporal(x_ref, cond_hbm, w_hbm, o_hbm, cond_ref, w_s, mod_s, p_s, o_s, sem):
    frames, count, width = x_ref.shape
    half = width // 2
    c_in = pltpu.make_async_copy(cond_hbm, cond_ref, sem.at[7])
    c_in.start()
    w_in = []
    for i in range(3):
        copy = pltpu.make_async_copy(
            w_hbm.at[:, pl.ds(i * width + half, half)], w_s.at[:, pl.ds(i * half, half)], sem.at[i]
        )
        copy.start()
        w_in.append(copy)
    c_in.wait()
    shift = cond_ref[0:1, :]
    gain = 1.0 + cond_ref[1:2, :]
    for f in range(0, frames, 2):
        piece = x_ref[f : f + 2].reshape(2 * count, width).astype(F32)
        mod_s[f * count : (f + 2) * count, :] = modulate(piece, shift, gain)
    for i in range(3):
        w_in[i].wait()
        cs = slice(i * half, (i + 1) * half)
        p_s[:, :, cs] = dot(mod_s[...], w_s[:, cs]).astype(BF16).reshape(frames, count, half)
    group = 128 // frames
    scale = 1.0 / jnp.sqrt(F32(HD))
    ri = lax.broadcasted_iota(jnp.int32, (128, 128), 0) % group
    ci = lax.broadcasted_iota(jnp.int32, (128, 128), 1) % group
    same = ri == ci
    outs = []
    for t in range(count // group):
        ts = slice(t * group, (t + 1) * group)

        def part(i, h):
            lo = i * half + h * HD
            return p_s[:, ts, lo : lo + HD].reshape(128, HD)

        heads = range(SHEADS)
        ss = [jnp.where(same, dot_t(part(0, h), part(1, h)) * scale, NEG) for h in heads]
        es = [jnp.exp(s - jnp.max(s, axis=-1, keepdims=True)) for s in ss]
        ws = [e * (1.0 / jnp.sum(e, axis=-1, keepdims=True)) for e in es]
        his = [w.astype(BF16) for w in ws]
        los = [(w - hi.astype(F32)).astype(BF16) for w, hi in zip(ws, his)]
        for h in heads:
            o = dot(his[h], part(2, h)) + dot(los[h], part(2, h))
            o_s[:, ts, h * HD : (h + 1) * HD] = o.astype(BF16).reshape(frames, group, HD)
        out = pltpu.make_async_copy(o_s.at[:, ts], o_hbm.at[:, ts], sem.at[3 + t])
        out.start()
        outs.append(out)
    for out in outs:
        out.wait()


def temporal_out(t_hbm, w_hbm, x_hbm, cond_hbm, o_hbm, t_s, w_s, x_s, cond_ref, o_s, sem):
    tokens, width = x_s.shape
    half = width // 2
    copies = [
        (t_hbm, t_s),
        (w_hbm.at[pl.ds(half, half)], w_s),
        (cond_hbm, cond_ref),
        (x_hbm.at[0], x_s),
    ]
    copies = [pltpu.make_async_copy(a, b, sem.at[i]) for i, (a, b) in enumerate(copies)]
    for c in copies:
        c.start()
    for c in copies:
        c.wait()
    gate = cond_ref[2:3, :]
    heads = t_s[...].reshape(tokens, half)
    quarter = width // 4
    outs = []
    for i in range(4):
        cs = slice(i * quarter, (i + 1) * quarter)
        o_s[:, cs] = x_s[:, cs].astype(F32) + gate[:, cs] * dot(heads, w_s[:, cs])
        out = pltpu.make_async_copy(o_s.at[:, cs], o_hbm.at[:, cs], sem.at[4 + i])
        out.start()
        outs.append(out)
    for out in outs:
        out.wait()


def finish(nb_hbm, cnt_hbm, acc_hbm, cond_hbm, slot_hbm, q_hbm, kv_hbm, left_ref, right_ref, w_hbm, o_hbm,
           nb_ref, cnt_ref, cond_ref, slot_ref, q_ref, win, blk_s, acc_s, w_s, o_s, sem):
    tokens, width = acc_s.shape
    half = width // 2
    copies = [
        (slot_hbm, slot_ref),
        (nb_hbm, nb_ref),
        (cnt_hbm, cnt_ref),
        (q_hbm, q_ref),
        (kv_hbm, win.at[pl.ds(tokens, tokens)]),
        (cond_hbm, cond_ref),
        (w_hbm.at[pl.ds(0, half)], w_s),
        (acc_hbm, acc_s),
    ]
    copies = [pltpu.make_async_copy(a, b, sem.at[i]) for i, (a, b) in enumerate(copies)]
    for c in copies[:6]:
        c.start()
    win[:tokens, :] = left_ref[...]
    win[2 * tokens :, :] = right_ref[...]
    copies[0].wait()
    tok = lax.broadcasted_iota(jnp.int32, (tokens, tokens), 0)
    unperm = (tok == slot_ref[...]).astype(F32).astype(BF16)
    scale = 1.0 / jnp.sqrt(F32(HD))
    total = 12 * NB
    for c in copies[1:6]:
        c.wait()
    for c in copies[6:]:
        c.start()
    first = nb_ref[0, 0]

    def select(j):
        starts = []
        lane = lax.broadcasted_iota(jnp.int32, (BLK, MAXNB * BLK), 1)
        keep = lane < cnt_ref[j] * BLK
        for n in range(MAXNB):
            at = lax.rem(nb_ref[j, n] - first + NB + total, total)
            at = jnp.minimum(at, 3 * NB - 1)
            starts.append(pl.multiple_of(at * BLK, BLK))

        def listed(lo):
            return jnp.concatenate([win[pl.ds(at, BLK), lo : lo + HD] for at in starts], axis=0)

        return slice(j * BLK, (j + 1) * BLK), keep, listed

    def score(item):
        (rows, keep, listed), h = item
        return jnp.where(keep, dot_t(q_ref[rows, h * HD : (h + 1) * HD], listed(h * HD)), NEG)

    items = [(sel, h) for sel in map(select, range(NB)) for h in range(SHEADS)]
    step = 2
    now = [score(item) for item in items[:step]]
    for g in range(0, len(items), step):
        ahead = [score(item) for item in items[g + step : g + 2 * step]]
        tops = [jnp.max(s, axis=-1, keepdims=True) for s in now]
        es = [jnp.exp2((s - top) * (scale * LOG2E)) for s, top in zip(now, tops)]
        invs = [1.0 / jnp.sum(e, axis=-1, keepdims=True) for e in es]
        for ((rows, _, listed), h), e, inv in zip(items[g : g + step], es, invs):
            o = dot(e.astype(BF16), listed(half + h * HD)) * inv
            blk_s[rows, h * HD : (h + 1) * HD] = o.astype(BF16)
        now = ahead
    copies[6].wait()
    copies[7].wait()
    gate = cond_ref[2:3, :]
    outs = []
    sp = dot(unperm, blk_s[...]).astype(BF16)
    quarter = width // 4
    for i in range(4):
        cs = slice(i * quarter, (i + 1) * quarter)
        o_s[:, cs] = (acc_s[:, cs] + gate[:, cs] * dot(sp, w_s[:, cs])).astype(BF16)
        out = pltpu.make_async_copy(o_s.at[:, cs], o_hbm.at[0, :, cs], sem.at[8 + i])
        out.start()
        outs.append(out)
    for out in outs:
        out.wait()


HB = pl.BlockSpec(memory_space=pltpu.HBM)
VM = pl.BlockSpec(memory_space=pltpu.VMEM)
DMA = pltpu.SemaphoreType.DMA


def near(x):
    return pltpu.with_memory_space_constraint(x, pltpu.VMEM)


def far(x):
    return pltpu.with_memory_space_constraint(x, pltpu.HBM)


def call(kernel, ins, outs, shapes, scratch):
    return pl.pallas_call(
        kernel,
        out_shape=shapes,
        in_specs=ins,
        out_specs=outs,
        scratch_shapes=scratch,
        name=kernel.__name__,
    )


def body(latent, cond, w_qkv, w_out, slot, neighbours, counts):
    tokens, width = latent.shape[1], latent.shape[2]
    half = width // 2
    per = tokens // CLIP
    slot_row = slot.reshape(1, tokens)
    arr = jax.ShapeDtypeStruct
    room = lambda *shape: pltpu.VMEM(shape, BF16)
    seen = lax.all_to_all(latent.reshape(CLIP, per, width), "member", 0, 0, tiled=True)
    kv, mod = call(
        spatial_keyval,
        [HB, HB, HB, HB],
        (HB, HB),
        (arr((tokens, width), BF16), arr((tokens, width), BF16)),
        [
            pltpu.VMEM((3, width), F32),
            pltpu.VMEM((1, tokens), jnp.int32),
            room(tokens, width),
            room(width, width),
            room(tokens, width),
            room(tokens, width),
            DMA((10,)),
        ],
    )(latent, cond, slot_row, w_qkv)
    count = lax.axis_size("space")
    left = lax.ppermute(kv, "space", [(i, (i + 1) % count) for i in range(count)])
    right = lax.ppermute(kv, "space", [((i + 1) % count, i) for i in range(count)])
    q = call(
        spatial_query,
        [HB, HB],
        VM,
        arr((tokens, half), BF16),
        [room(tokens, width), room(width, half), DMA((2,))],
    )(mod, w_qkv)
    t_out = call(
        temporal,
        [VM, HB, HB],
        HB,
        arr((CLIP, per, half), BF16),
        [
            pltpu.VMEM((3, width), F32),
            room(width, 3 * half),
            room(tokens, width),
            room(CLIP, per, 3 * half),
            room(CLIP, per, half),
            DMA((8,)),
        ],
    )(near(seen), cond, w_qkv)
    back = far(lax.all_to_all(t_out, "member", 0, 0, tiled=True))
    acc = call(
        temporal_out,
        [HB, HB, HB, HB],
        HB,
        arr((tokens, width), F32),
        [
            room(CLIP, per, half),
            room(half, width),
            room(tokens, width),
            pltpu.VMEM((3, width), F32),
            pltpu.VMEM((tokens, width), F32),
            DMA((8,)),
        ],
    )(back, w_out, latent, cond)
    return call(
        finish,
        [HB] * 7 + [VM, VM, HB],
        HB,
        arr((1, tokens, width), BF16),
        [
            pltpu.SMEM((NB, MAXNB), jnp.int32),
            pltpu.SMEM((NB,), jnp.int32),
            pltpu.VMEM((3, width), F32),
            pltpu.VMEM((1, tokens), jnp.int32),
            room(tokens, half),
            room(3 * tokens, width),
            room(tokens, half),
            pltpu.VMEM((tokens, width), F32),
            room(half, width),
            room(tokens, width),
            DMA((12,)),
        ],
    )(neighbours, counts, acc, cond, slot_row, q, kv, near(left), near(right), w_out)


def solution(mesh):
    devices = mesh.devices
    spaces, frames = devices.shape
    fine = Mesh(devices.reshape(spaces, frames // CLIP, CLIP), ("space", "clip", "member"))
    whole = ("clip", "member")
    in_specs = (P(whole, "space", None), P(), P(), P(), P("space"), P("space", None), P("space"))
    out_specs = P(whole, "space", None)
    return jax.shard_map(body, mesh=fine, in_specs=in_specs, out_specs=out_specs, check_vma=False)
```
